1024 devices in a mesh: ctx: 128 (over y_lo, z, core), ch: 8 (over y_hi, x).
Axes of the slice: x: 4, y: 8 (y_hi: 2, y_lo: 4; y = y_hi * 4 + y_lo), z: 16, core: 2. Of those that a mesh axis runs over, the one named last changes fastest.
Arguments:
- query: bfloat16 [16384, 8192], P('ctx', 'ch'), may hold values from -6 to 6
- key: bfloat16 [16384, 8192], P('ctx', 'ch'), may hold values from -6 to 6
- value: bfloat16 [16384, 8192], P('ctx', 'ch'), may hold values from -6 to 6
- cotangent: bfloat16 [16384, 8192], P('ctx', 'ch'), may hold values from -6 to 6
- decay: float32 [4, 8192], P(None, 'ch'), may hold values from 0.95 to 1, as said below
- residue: float32 [4, 8192], P(None, 'ch'), may hold values from -3 to 3
- skip: float32 [8192], P('ch'), may hold values from -4 to 4
Outputs:
- output: bfloat16 [16384, 8192], P('ctx', 'ch')
- query_grad: bfloat16 [16384, 8192], P('ctx', 'ch')
- key_grad: bfloat16 [16384, 8192], P('ctx', 'ch')
- value_grad: bfloat16 [16384, 8192], P('ctx', 'ch')
- residue_grad: float32 [4, 8192], P(None, 'ch')
- skip_grad: float32 [8192], P('ch')
The draws below stay inside these ranges and needn't reach their ends.
Inputs may be any that keep to these rules, and one draw needn't show every extreme that they name: decay lies below 1.
All inputs are finite; a program needn't handle non-finite values.
Results may differ from the reference program's by a relative error of at most 0.0012.
Values sent between devices are 32-bit elements; how exact they have to be, the bound alone decides.
No kernel may reach another device: no remote copies, remote signals or barrier semaphores. Data moves between devices by JAX's collectives and lax.ppermute only.
A program may use at most 32 MiB of HBM per device.

```python
import math
import jax
import jax.numpy as jnp
from jax import lax

D = 8192
MODES = 4
SEQ = 16384


def draw_decay(key, part):
    first, second = jax.random.split(key, 2)
    slow_share = 0.5
    slow = jax.random.uniform(first, (MODES, D), jnp.float32) < slow_share
    ratio = jax.random.uniform(second, (MODES, D), jnp.float32)
    slow_low = math.log(0.1 / SEQ)
    slow_high = math.log(2.0 / SEQ)
    fast_high = math.log(0.05)
    slow_rate = jnp.exp(slow_low + ratio * (slow_high - slow_low))
    fast_rate = jnp.exp(slow_high + ratio * (fast_high - slow_high))
    rate = jnp.where(slow, slow_rate, fast_rate)
    return jnp.exp(-rate).astype(jnp.float32)


def steps_of(rng, shape, shards, low, top_value):
    def one(dim, parts):
        draws = jax.random.uniform(jax.random.fold_in(jax.random.fold_in(rng, 6), dim), (parts,), jnp.float32, low / len(shards), top_value / len(shards))
        return jnp.repeat(jnp.exp(draws), shape[dim] // parts).reshape((-1,) + (1,) * (len(shape) - dim - 1))

    level = one(*shards[0])
    for cut in shards[1:]:
        level = level * one(*cut)
    return level


def bell_draw(own_key, dims, scale, limit, cuts=(), kind=jnp.bfloat16):
    result = scale * jax.random.normal(own_key, dims, jnp.float32)
    if cuts:
        result = result * steps_of(own_key, dims, cuts, -0.22, 0.18)
    return jnp.clip(result, -limit, limit).astype(kind)


def setup_inputs(seed: int = 0) -> dict:
    arg_keys = jax.random.split(jax.random.key(seed), 8)
    return {
        "query": bell_draw(arg_keys[0], (SEQ, D), 1.0, 6.0, ((0, 128), (1, 8))),
        "key": bell_draw(arg_keys[1], (SEQ, D), 1.0, 6.0, ((0, 128), (1, 8))),
        "value": bell_draw(arg_keys[2], (SEQ, D), 1.0, 6.0, ((0, 128), (1, 8))),
        "cotangent": bell_draw(arg_keys[3], (SEQ, D), 1.0, 6.0, ((0, 128), (1, 8))),
        "decay": draw_decay(jax.random.fold_in(arg_keys[7], 71), 0),
        "residue": bell_draw(arg_keys[5], (MODES, D), 0.5, 3.0, ((1, 8),), jnp.float32),
        "skip": bell_draw(arg_keys[6], (D,), 1.0, 4.0, ((0, 8),), jnp.float32),
    }


def reference(query, key, value, cotangent, decay, residue, skip):
    inner = key.astype(jnp.float32) * value.astype(jnp.float32)
    grad_z = cotangent.astype(jnp.float32) * query.astype(jnp.float32)
    spread = jnp.sqrt((1.0 - decay) * (1.0 + decay))
    coeffs = residue * spread
    zero_state = jnp.zeros(decay.shape, jnp.float32)

    def forward(carry, inputs):
        state, total = carry
        inner_row, grad_row = inputs
        state = decay * state + inner_row[None, :]
        total = total + grad_row[None, :] * state
        return ((state, total), lax.optimization_barrier(jnp.sum(coeffs * state, axis=0)))
    (last_state, totals), mixed = lax.scan(forward, (zero_state, zero_state), (inner, grad_z))
    mixed_z = mixed + skip[None, :] * inner

    def backward(state, grad_row):
        state = decay * state + grad_row[None, :]
        return (state, lax.optimization_barrier(jnp.sum(coeffs * state, axis=0)))
    first_state, back_mixed = lax.scan(backward, zero_state, grad_z, reverse=True)
    inner_grad = back_mixed + skip[None, :] * grad_z
    scale = 1.0 / math.sqrt(SEQ)
    output = (query.astype(jnp.float32) * mixed_z).astype(jnp.bfloat16)
    query_grad = (cotangent.astype(jnp.float32) * mixed_z).astype(jnp.bfloat16)
    key_grad = (inner_grad * value.astype(jnp.float32)).astype(jnp.bfloat16)
    value_grad = (inner_grad * key.astype(jnp.float32)).astype(jnp.bfloat16)
    residue_grad = spread * totals * scale
    skip_grad = lax.optimization_barrier(jnp.sum(grad_z * inner, axis=0)) * scale
    return (output, query_grad, key_grad, value_grad, residue_grad, skip_grad)
```

```python
import math

import jax
import jax.numpy as jnp
from jax import lax
from jax.experimental import pallas as pl
from jax.experimental.pallas import tpu as pltpu
from jax.sharding import Mesh, PartitionSpec as P

MODES = 4
SEGS = 8
LANES = 128
WIDTH = 256


def shifted(x, amount, row):
    rolled = pltpu.roll(x, amount % SEGS, axis=0)
    inside = row >= amount if amount > 0 else row < SEGS + amount
    return jnp.where(inside, rolled, 0.0)


def segment_scan(x, factor, direction, row):
    total = shifted(x, direction, row)
    step = 1
    while step < SEGS:
        total = total + factor * shifted(total, direction * step, row)
        factor = factor * factor
        step *= 2
    return total


def summarize(
    query, key, value, cotangent, decay, log_decay, coeffs, skip,
    summary, forward, backward, entered, left, inner_buf, grad_buf,
):
    steps = forward.shape[0]
    row = lax.broadcasted_iota(jnp.int32, (SEGS, LANES), 0)
    for block in range(forward.shape[2] // LANES):
        cols = slice(block * LANES, (block + 1) * LANES)
        inner_buf[block] = key[:, cols].astype(jnp.float32) * value[:, cols].astype(jnp.float32)
        grad_buf[block] = cotangent[:, cols].astype(jnp.float32) * query[:, cols].astype(jnp.float32)

        def spread_row(ref, n):
            return jnp.broadcast_to(ref[n : n + 1, cols], (SEGS, LANES))

        a = [spread_row(decay, n) for n in range(MODES)]
        coef = [spread_row(coeffs, n) for n in range(MODES)]
        direct = spread_row(skip, 0)
        state = [jnp.zeros((SEGS, LANES), jnp.float32) for _ in range(MODES)]
        product = [jnp.zeros((SEGS, LANES), jnp.float32) for _ in range(MODES)]
        plain = jnp.zeros((SEGS, LANES), jnp.float32)
        for i in range(steps):
            u = inner_buf[block, pl.ds(i, SEGS, stride=steps), :]
            g = grad_buf[block, pl.ds(i, SEGS, stride=steps), :]
            mixed = direct * u
            plain = plain + g * u
            for n in range(MODES):
                state[n] = a[n] * state[n] + u
                product[n] = product[n] + g * state[n]
                mixed = mixed + coef[n] * state[n]
            forward[i, :, cols] = mixed
        back = [jnp.zeros((SEGS, LANES), jnp.float32) for _ in range(MODES)]
        for i in reversed(range(steps)):
            g = grad_buf[block, pl.ds(i, SEGS, stride=steps), :]
            mixed = direct * g
            for n in range(MODES):
                back[n] = a[n] * back[n] + g
                mixed = mixed + coef[n] * back[n]
            backward[i, :, cols] = mixed
        for n in range(MODES):
            factor = jnp.exp(float(steps) * spread_row(log_decay, n))
            before = segment_scan(state[n], factor, 1, row)
            after = segment_scan(back[n], factor, -1, row)
            entered[n, :, cols] = before
            left[n, :, cols] = after
            summary[n : n + 1, cols] = (factor * before + state[n])[SEGS - 1 :]
            summary[MODES + n : MODES + n + 1, cols] = (factor * after + back[n])[:1]
            summary[2 * MODES + n : 2 * MODES + n + 1, cols] = jnp.sum(
                product[n] + a[n] * back[n] * before, axis=0, keepdims=True
            )
        summary[3 * MODES : 3 * MODES + 1, cols] = jnp.sum(plain, axis=0, keepdims=True)
        summary[3 * MODES + 1 :, cols] = jnp.zeros((MODES - 1, LANES), jnp.float32)


def finish(
    query, key, value, cotangent, decay, log_decay, coeffs, carry_in, carry_back,
    forward, backward, entered, left,
    output, query_grad, key_grad, value_grad, mixed_buf, back_buf,
):
    steps = forward.shape[0]
    row = lax.broadcasted_iota(jnp.int32, (SEGS, LANES), 0).astype(jnp.float32)
    for block in range(forward.shape[2] // LANES):
        cols = slice(block * LANES, (block + 1) * LANES)

        def spread_row(ref, n):
            return jnp.broadcast_to(ref[n : n + 1, cols], (SEGS, LANES))

        a, ahead, behind = [], [], []
        for n in range(MODES):
            a.append(spread_row(decay, n))
            log_a = spread_row(log_decay, n)
            first = spread_row(coeffs, n) * a[n]
            falling = jnp.exp(float(steps) * row * log_a)
            rising = jnp.exp(float(steps) * (SEGS - 1.0 - row) * log_a)
            ahead.append(first * (entered[n, :, cols] + falling * spread_row(carry_in, n)))
            behind.append(first * (left[n, :, cols] + rising * spread_row(carry_back, n)))
        for i in range(steps):
            mixed = forward[i, :, cols]
            for n in range(MODES):
                mixed = mixed + ahead[n]
                ahead[n] = ahead[n] * a[n]
            mixed_buf[block, pl.ds(i, SEGS, stride=steps), :] = mixed
        for i in reversed(range(steps)):
            mixed = backward[i, :, cols]
            for n in range(MODES):
                mixed = mixed + behind[n]
                behind[n] = behind[n] * a[n]
            back_buf[block, pl.ds(i, SEGS, stride=steps), :] = mixed
        mixed_z = mixed_buf[block]
        inner_grad = back_buf[block]
        output[:, cols] = (query[:, cols].astype(jnp.float32) * mixed_z).astype(output.dtype)
        query_grad[:, cols] = (cotangent[:, cols].astype(jnp.float32) * mixed_z).astype(output.dtype)
        key_grad[:, cols] = (inner_grad * value[:, cols].astype(jnp.float32)).astype(output.dtype)
        value_grad[:, cols] = (inner_grad * key[:, cols].astype(jnp.float32)).astype(output.dtype)


def rows_spec(rows):
    return pl.BlockSpec((rows, WIDTH), lambda i: (0, i))


def deep_spec(depth):
    return pl.BlockSpec((depth, SEGS, WIDTH), lambda i: (0, 0, i))


def parts_of(summary):
    return (
        summary[:MODES],
        summary[MODES : 2 * MODES],
        summary[2 * MODES : 3 * MODES],
        summary[3 * MODES : 3 * MODES + 1],
    )


def joined(parts, decay, span):
    tail, head, products, plain = parts[0]
    reach = span
    for later_tail, later_head, later_products, later_plain in parts[1:]:
        products = products + later_products + decay * later_head * tail
        plain = plain + later_plain
        tail = span * tail + later_tail
        head = head + reach * later_head
        reach = reach * span
    return tail, head, products, plain


def around(parts, place, span):
    before = jnp.zeros_like(span)
    after = jnp.zeros_like(span)
    for j in range(len(parts)):
        before = jnp.where(j < place, span * before + parts[j][0], before)
    for j in reversed(range(len(parts))):
        after = jnp.where(j > place, span * after + parts[j][1], after)
    return before, after


def exchanged(summary, axis, size):
    return lax.all_to_all(
        jnp.broadcast_to(summary[None], (size, *summary.shape)), axis, 0, 0, tiled=True
    )


def local(query, key, value, cotangent, decay, residue, skip):
    tokens, width = query.shape
    steps = tokens // SEGS
    log_decay = jnp.log1p(decay - 1.0)
    spread = jnp.sqrt((1.0 - decay) * (1.0 + decay))
    coeffs = residue * spread
    skip_row = skip[None, :]
    grid = (width // WIDTH,)
    wide = rows_spec(tokens)
    modes = rows_spec(MODES)
    shape_of = jax.ShapeDtypeStruct
    f32 = jnp.float32
    summary, forward, backward, entered, left = pl.pallas_call(
        summarize,
        grid=grid,
        in_specs=[wide] * 4 + [modes] * 3 + [rows_spec(1)],
        out_specs=[rows_spec(4 * MODES), deep_spec(steps), deep_spec(steps), deep_spec(MODES), deep_spec(MODES)],
        out_shape=[
            shape_of((4 * MODES, width), f32),
            shape_of((steps, SEGS, width), f32),
            shape_of((steps, SEGS, width), f32),
            shape_of((MODES, SEGS, width), f32),
            shape_of((MODES, SEGS, width), f32),
        ],
        scratch_shapes=[pltpu.VMEM((WIDTH // LANES, tokens, LANES), f32)] * 2,
        name="summarize",
    )(query, key, value, cotangent, decay, log_decay, coeffs, skip_row)

    half = width // 2
    core = lax.axis_index("core")
    pair = lax.all_gather(summary, "core")
    own = lax.dynamic_slice_in_dim(pair, core * half, half, 2)
    own_decay = lax.dynamic_slice_in_dim(decay, core * half, half, 1)
    own_log = lax.dynamic_slice_in_dim(log_decay, core * half, half, 1)
    span = jnp.exp(tokens * own_log)
    stretch = tokens * 2
    stretches = joined([parts_of(own[0]), parts_of(own[1])], own_decay, span)
    inward, outward = jnp.zeros_like(own_log), jnp.zeros_like(own_log)
    reach_in, reach_out = jnp.ones_like(own_log), jnp.ones_like(own_log)
    for axis in ("z_lo", "z_hi", "y"):
        size = lax.axis_size(axis)
        place = lax.axis_index(axis)
        block = jnp.concatenate([*stretches, jnp.zeros((MODES - 1, half), f32)], axis=0)
        everyone = exchanged(block, axis, size)
        parts = [parts_of(everyone[j]) for j in range(size)]
        span = jnp.exp(stretch * own_log)
        before, after = around(parts, place, span)
        inward = inward + reach_in * before
        outward = outward + reach_out * after
        reach_in = reach_in * jnp.exp((stretch * place).astype(f32) * own_log)
        reach_out = reach_out * jnp.exp((stretch * (size - 1 - place)).astype(f32) * own_log)
        stretches = joined(parts, own_decay, span)
        stretch *= size
    _, _, products, plain = stretches
    final = jnp.concatenate([inward, outward, products, plain, jnp.zeros((MODES - 1, half), f32)], axis=0)
    final = lax.all_gather(final, "core", axis=1, tiled=True)
    inward, outward, products, plain = parts_of(final)
    span = jnp.exp(tokens * log_decay)
    first = core == 0
    carry_in = jnp.where(first, inward, pair[0, :MODES] + span * inward)
    carry_back = jnp.where(first, pair[1, MODES : 2 * MODES] + span * outward, outward)

    bf16 = shape_of((tokens, width), query.dtype)
    output, query_grad, key_grad, value_grad = pl.pallas_call(
        finish,
        grid=grid,
        in_specs=[wide] * 4 + [modes] * 5 + [deep_spec(steps), deep_spec(steps), deep_spec(MODES), deep_spec(MODES)],
        out_specs=[wide] * 4,
        out_shape=[bf16] * 4,
        scratch_shapes=[pltpu.VMEM((WIDTH // LANES, tokens, LANES), f32)] * 2,
        name="finish",
    )(query, key, value, cotangent, decay, log_decay, coeffs, carry_in, carry_back, forward, backward, entered, left)
    scale = 1.0 / math.sqrt(tokens * lax.axis_size(("y", "z_hi", "z_lo", "core")))
    return (output, query_grad, key_grad, value_grad, spread * products * scale, plain[0] * scale)


def solution(mesh):
    context = ("y", "z_hi", "z_lo", "core")
    rows, columns = mesh.devices.shape
    fine = Mesh(mesh.devices.reshape(rows // 32, 4, 4, 2, columns), (*context, "ch"))
    wide, modes, flat = P(context, "ch"), P(None, "ch"), P("ch")
    return jax.shard_map(
        local,
        mesh=fine,
        in_specs=(wide, wide, wide, wide, modes, modes, flat),
        out_specs=(wide, wide, wide, wide, modes, flat),
        check_vma=False,
    )
```

```python
import math

import jax
import jax.numpy as jnp
from jax import lax
from jax.experimental import pallas as pl
from jax.experimental.pallas import tpu as pltpu
from jax.sharding import Mesh, PartitionSpec as P

MODES = 4
SEGS = 8
LANES = 128
TOGETHER = 2
MIX_WIDTH = 512
VMEM_LIMIT = 16 * 1024 * 1024


def shifted(x, amount, row):
    rolled = pltpu.roll(x, amount % SEGS, axis=0)
    inside = row >= amount if amount > 0 else row < SEGS + amount
    return jnp.where(inside, rolled, 0.0)


def segment_scan(x, factor, direction, row):
    total = shifted(x, direction, row)
    step = 1
    while step < SEGS:
        total = total + factor * shifted(total, direction * step, row)
        factor = factor * factor
        step *= 2
    return total


def columns(block):
    return pl.ds(pl.multiple_of(block * LANES, LANES), LANES)


def over_blocks(count, one):
    def trip(step, carry):
        for k in range(TOGETHER):
            one(step * TOGETHER + k, k)
        return carry

    lax.fori_loop(0, count // TOGETHER, trip, 0)


def spread_out(ref, n, cols):
    return jnp.broadcast_to(ref[n : n + 1, cols], (SEGS, LANES))


def mode_weights(decay, residue, cols):
    a = [spread_out(decay, n, cols) for n in range(MODES)]
    return a, [spread_out(residue, n, cols) * jnp.sqrt((1.0 - x) * (1.0 + x)) for n, x in enumerate(a)]


def squared(x, times):
    for _ in range(times):
        x = x * x
    return x


def loaded(query, key, value, cotangent, inner_buf, grad_buf, block, cols):
    inner_buf[block] = key[:, cols].astype(jnp.float32) * value[:, cols].astype(jnp.float32)
    grad_buf[block] = cotangent[:, cols].astype(jnp.float32) * query[:, cols].astype(jnp.float32)


def summarize(
    query, key, value, cotangent, decay_away,
    summary, query_held, key_held, value_held, cotangent_held, inner_buf, grad_buf, decay, arrived,
):
    tokens, width = query.shape
    steps = tokens // SEGS
    held = (query_held, key_held, value_held, cotangent_held)
    row = lax.broadcasted_iota(jnp.int32, (SEGS, LANES), 0)
    zero = jnp.zeros((SEGS, LANES), jnp.float32)

    copies = [
        pltpu.make_async_copy(ref, to, arrived.at[n])
        for n, (ref, to) in enumerate(zip((decay_away, query, key, value, cotangent), (decay, *held)))
    ]
    for copy in copies:
        copy.start()
    for copy in copies:
        copy.wait()

    def one(block, buf):
        cols = columns(block)
        loaded(*held, inner_buf, grad_buf, buf, cols)
        a = [spread_out(decay, n, cols) for n in range(MODES)]
        state, back, product, plain = [zero] * MODES, [zero] * MODES, [zero] * MODES, zero
        power = [zero + 1.0] * MODES
        for i in range(steps):
            u = inner_buf[buf, pl.ds(i, SEGS, stride=steps), :]
            g = grad_buf[buf, pl.ds(i, SEGS, stride=steps), :]
            plain = plain + g * u
            for n in range(MODES):
                state[n] = a[n] * state[n] + u
                product[n] = product[n] + g * state[n]
                back[n] = back[n] + power[n] * g
                power[n] = power[n] * a[n]
        for n in range(MODES):
            factor = power[n]
            before = segment_scan(state[n], factor, 1, row)
            after = segment_scan(back[n], factor, -1, row)
            summary[block, n : n + 1] = (factor * before + state[n])[SEGS - 1 :]
            summary[block, MODES + n : MODES + n + 1] = (factor * after + back[n])[:1]
            summary[block, 2 * MODES + n : 2 * MODES + n + 1] = jnp.sum(
                product[n] + a[n] * back[n] * before, axis=0, keepdims=True
            )
        summary[block, 3 * MODES : 3 * MODES + 1] = jnp.sum(plain, axis=0, keepdims=True)
        summary[block, 3 * MODES + 1 :] = jnp.zeros((MODES - 1, LANES), jnp.float32)

    over_blocks(width // LANES, one)


def mix(
    query, key, value, cotangent, decay, residue, skip,
    forward, backward, entered, left, decays, inner_buf, grad_buf,
):
    steps = forward.shape[0]
    doublings = steps.bit_length() - 1
    row = lax.broadcasted_iota(jnp.int32, (SEGS, LANES), 0)
    zero = jnp.zeros((SEGS, LANES), jnp.float32)
    for block in range(forward.shape[2] // LANES):
        cols = slice(block * LANES, (block + 1) * LANES)
        loaded(query, key, value, cotangent, inner_buf, grad_buf, block, cols)
        a, coef = mode_weights(decay, residue, cols)
        direct = spread_out(skip, 0, cols)
        state, back = [zero] * MODES, [zero] * MODES
        for i in range(steps):
            u = inner_buf[block, pl.ds(i, SEGS, stride=steps), :]
            mixed = direct * u
            for n in range(MODES):
                state[n] = a[n] * state[n] + u
                mixed = mixed + coef[n] * state[n]
            forward[i, :, cols] = mixed
        for i in reversed(range(steps)):
            g = grad_buf[block, pl.ds(i, SEGS, stride=steps), :]
            mixed = direct * g
            for n in range(MODES):
                back[n] = a[n] * back[n] + g
                mixed = mixed + coef[n] * back[n]
            backward[i, :, cols] = mixed
        for n in range(MODES):
            factor = squared(a[n], doublings)
            first = coef[n] * a[n]
            entered[n, :, cols] = first * segment_scan(state[n], factor, 1, row)
            left[n, :, cols] = first * segment_scan(back[n], factor, -1, row)
        decays[block] = decay[:, cols]


def finish(
    query, key, value, cotangent, decay, residue, carried,
    forward, backward, entered, left,
    output, query_grad, key_grad, value_grad, residue_grad, skip_grad, mixed_buf, back_buf,
):
    steps = forward.shape[0]
    doublings = steps.bit_length() - 1
    row = lax.broadcasted_iota(jnp.int32, (SEGS, LANES), 0)
    for block in range(forward.shape[2] // LANES):
        cols = slice(block * LANES, (block + 1) * LANES)
        a, coef = mode_weights(decay, residue, cols)
        ahead, behind = [], []
        for n in range(MODES):
            first = coef[n] * a[n]
            factor = squared(a[n], doublings)
            falling, rising = 1.0, 1.0
            for bit in (1, 2, 4):
                falling = falling * jnp.where(row & bit != 0, factor, 1.0)
                rising = rising * jnp.where(row & bit != 0, 1.0, factor)
                factor = factor * factor
            carry_in = jnp.broadcast_to(carried[block, n : n + 1], (SEGS, LANES))
            carry_back = jnp.broadcast_to(carried[block, MODES + n : MODES + n + 1], (SEGS, LANES))
            ahead.append(entered[n, :, cols] + first * falling * carry_in)
            behind.append(left[n, :, cols] + first * rising * carry_back)
        for i in range(steps):
            mixed = forward[i, :, cols]
            for n in range(MODES):
                mixed = mixed + ahead[n]
                ahead[n] = ahead[n] * a[n]
            mixed_buf[block, pl.ds(i, SEGS, stride=steps), :] = mixed
        for i in reversed(range(steps)):
            mixed = backward[i, :, cols]
            for n in range(MODES):
                mixed = mixed + behind[n]
                behind[n] = behind[n] * a[n]
            back_buf[block, pl.ds(i, SEGS, stride=steps), :] = mixed
        mixed_z = mixed_buf[block]
        inner_grad = back_buf[block]
        output[:, cols] = (query[:, cols].astype(jnp.float32) * mixed_z).astype(output.dtype)
        query_grad[:, cols] = (cotangent[:, cols].astype(jnp.float32) * mixed_z).astype(output.dtype)
        key_grad[:, cols] = (inner_grad * value[:, cols].astype(jnp.float32)).astype(output.dtype)
        value_grad[:, cols] = (inner_grad * key[:, cols].astype(jnp.float32)).astype(output.dtype)
        residue_grad[:, cols] = carried[block, 2 * MODES : 3 * MODES]
        skip_grad[:, cols] = carried[block, 3 * MODES : 3 * MODES + 1]


def rows_spec(rows):
    return pl.BlockSpec((rows, MIX_WIDTH), lambda i: (0, i))


def deep_spec(depth):
    return pl.BlockSpec((depth, SEGS, MIX_WIDTH), lambda i: (0, 0, i))


def per_block(rows):
    return pl.BlockSpec((MIX_WIDTH // LANES, rows, LANES), lambda i: (i, 0, 0))


def parts_of(gathered):
    return (
        gathered[:, :MODES],
        gathered[:, MODES : 2 * MODES],
        gathered[:, 2 * MODES : 3 * MODES],
        gathered[:, 3 * MODES : 3 * MODES + 1],
    )


def running(each, spans, reverse):
    step = 1
    for span in spans:
        rest = jnp.zeros((step, *each.shape[1:]), each.dtype)
        moved = jnp.concatenate([each[step:], rest] if reverse else [rest, each[:-step]], axis=0)
        each = each + span * moved
        step *= 2
    return each


def whole_of(parts, decay, spans):
    tails, heads, products, plains = parts
    count = tails.shape[0]
    tail, head, product, plain = tails[0], heads[count - 1], products[0], plains[0]
    for j in range(1, count):
        product = product + products[j] + decay * heads[j] * tail
        plain = plain + plains[j]
        tail = spans[0] * tail + tails[j]
        head = spans[0] * head + heads[count - 1 - j]
    return tail, head, product, plain


def weighted(weights, each):
    total = weights[0] * each[0]
    for j in range(1, each.shape[0]):
        total = total + weights[j] * each[j]
    return total


def padded(parts):
    plain = parts[3]
    rest = jnp.zeros((*plain.shape[:-2], MODES - 1, LANES), plain.dtype)
    return jnp.concatenate([*parts, rest], axis=-2)


def exchanged(blocks, axis):
    return lax.all_to_all(blocks, axis, 0, 0, tiled=True)


def local(query, key, value, cotangent, decay, residue, skip):
    tokens, width = query.shape
    steps = tokens // SEGS
    grid = (width // MIX_WIDTH,)
    wide, modes = rows_spec(tokens), rows_spec(MODES)
    shape_of, f32 = jax.ShapeDtypeStruct, jnp.float32
    buffers = [pltpu.VMEM((MIX_WIDTH // LANES, tokens, LANES), f32)] * 2
    small = pltpu.CompilerParams(vmem_limit_bytes=VMEM_LIMIT)
    far_off, whole = pl.BlockSpec(memory_space=pltpu.HBM), pl.BlockSpec(memory_space=pltpu.VMEM)
    blocks = width // LANES
    away = [pltpu.with_memory_space_constraint(x, pltpu.HBM) for x in (query, key, value, cotangent, decay)]
    summary, *sources = pl.pallas_call(
        summarize,
        in_specs=[far_off] * 5,
        out_specs=[whole] * 5,
        out_shape=[shape_of((blocks, 4 * MODES, LANES), f32)] + [pltpu.VMEM((tokens, width), query.dtype)] * 4,
        scratch_shapes=[pltpu.VMEM((TOGETHER, tokens, LANES), f32)] * 2
        + [pltpu.VMEM((MODES, width), f32), pltpu.SemaphoreType.DMA((5,))],
        compiler_params=small,
        name="summarize",
    )(*away)
    deep = [steps, steps, MODES, MODES]
    forward, backward, entered, left, decays = pl.pallas_call(
        mix,
        grid=grid,
        in_specs=[wide] * 4 + [modes] * 2 + [rows_spec(1)],
        out_specs=[deep_spec(depth) for depth in deep]
        + [per_block(MODES)],
        out_shape=[shape_of((depth, SEGS, width), f32) for depth in deep] + [shape_of((blocks, MODES, LANES), f32)],
        scratch_shapes=buffers,
        compiler_params=small,
        cost_estimate=pl.CostEstimate(flops=40 * tokens * width, bytes_accessed=16 * tokens * width, transcendentals=0),
        name="mix",
    )(*sources, decay, residue, skip[None, :])

    near = ("z_lo", "core")
    own_decay = lax.dynamic_index_in_dim(decays, lax.axis_index(near), 0, False)
    log_decay = jnp.log1p(own_decay - 1.0)

    def power(counts):
        return jnp.exp(counts[:, None, None] * log_decay)

    def held(used, counts):
        return jnp.where(used[:, None, None], power(jnp.maximum(counts, 0).astype(f32)), 0.0)

    near_count = lax.axis_size(near)
    mid_count, far_count = lax.axis_size("z_hi"), lax.axis_size("y")
    mid_place, far_place = lax.axis_index("z_hi"), lax.axis_index("y")
    mid_length = tokens * near_count
    far_length = mid_length * mid_count
    near_place = jnp.arange(near_count)
    reach_in = power((tokens * near_place).astype(f32))
    reach_back = power((tokens * (near_count - 1 - near_place)).astype(f32))
    doublings = (near_count * mid_count * far_count).bit_length() - 1
    spans = power((tokens * (1 << jnp.arange(doublings))).astype(f32))
    near_steps = near_count.bit_length() - 1
    mid_steps = near_steps + mid_count.bit_length() - 1
    mid = jnp.arange(mid_count)
    mid_in = held(mid < mid_place, mid_length * (mid_place - 1 - mid))
    mid_back = held(mid > mid_place, mid_length * (mid - mid_place - 1))
    far = jnp.arange(far_count)
    far_in = held(far < far_place, far_length * (far_place - 1 - far) + mid_length * mid_place)
    far_back = held(far > far_place, far_length * (far - far_place - 1) + mid_length * (mid_count - 1 - mid_place))
    scale = 1.0 / math.sqrt(far_length * far_count)
    spread = jnp.sqrt((1.0 - own_decay) * (1.0 + own_decay)) * scale

    def shared(stretch, count, axis):
        return parts_of(exchanged(jnp.broadcast_to(padded(stretch)[None], (count, 4 * MODES, LANES)), axis))

    near_parts = exchanged(summary, near)
    (
        near_parts, forward, backward, entered, left, own_decay, spread,
        reach_in, reach_back, spans, mid_in, mid_back, far_in, far_back,
    ) = lax.optimization_barrier(
        (
            near_parts, forward, backward, entered, left, own_decay, spread,
            reach_in, reach_back, [spans[k] for k in range(doublings)], mid_in, mid_back, far_in, far_back,
        )
    )
    near_spans, mid_spans, far_spans = spans[:near_steps], spans[near_steps:mid_steps], spans[mid_steps:]
    parts = parts_of(near_parts)
    ahead, behind = running(parts[0], near_spans, False), running(parts[1], near_spans, True)
    rest = jnp.zeros((1, MODES, LANES), f32)
    near_before = jnp.concatenate([rest, ahead[:-1]], axis=0)
    near_after = jnp.concatenate([behind[1:], rest], axis=0)
    products = jnp.sum(parts[2] + own_decay * parts[1] * near_before, axis=0)
    stretch = (ahead[-1], behind[0], products, jnp.sum(parts[3], axis=0))
    near_before, near_after, stretch = lax.optimization_barrier((near_before, near_after, stretch))
    parts = shared(stretch, mid_count, "z_hi")
    entering, leaving = weighted(mid_in, parts[0]), weighted(mid_back, parts[1])
    stretch = whole_of(parts, own_decay, mid_spans)
    entering, leaving, stretch = lax.optimization_barrier((entering, leaving, stretch))
    parts = shared(stretch, far_count, "y")
    entering = entering + weighted(far_in, parts[0])
    leaving = leaving + weighted(far_back, parts[1])
    _, _, products, plain = whole_of(parts, own_decay, far_spans)
    everyone = (near_count, MODES, LANES)
    carried = padded(
        (
            near_before + reach_in * entering,
            near_after + reach_back * leaving,
            jnp.broadcast_to(spread * products, everyone),
            jnp.broadcast_to(scale * plain, (near_count, 1, LANES)),
        )
    )
    carried = exchanged(carried, near)

    bf16 = shape_of((tokens, width), query.dtype)
    *grads, skip_grad = pl.pallas_call(
        finish,
        grid=grid,
        in_specs=[wide] * 4 + [modes] * 2 + [per_block(4 * MODES)] + [deep_spec(depth) for depth in deep],
        out_specs=[wide] * 4 + [modes, rows_spec(1)],
        out_shape=[bf16] * 4 + [shape_of((MODES, width), f32), shape_of((1, width), f32)],
        scratch_shapes=buffers,
        compiler_params=small,
        name="finish",
    )(*sources, decay, residue, carried, forward, backward, entered, left)
    return (*grads, skip_grad[0])


def solution(mesh):
    context = ("y", "z_hi", "z_lo", "core")
    rows, columns = mesh.devices.shape
    fine = Mesh(mesh.devices.reshape(rows // 32, 4, 4, 2, columns), (*context, "ch"))
    wide, modes, flat = P(context, "ch"), P(None, "ch"), P("ch")
    return jax.shard_map(
        local,
        mesh=fine,
        in_specs=(wide, wide, wide, wide, modes, modes, flat),
        out_specs=(wide, wide, wide, wide, modes, flat),
        check_vma=False,
    )
```

```python
import math

import jax
import jax.numpy as jnp
from jax import lax
from jax.experimental import pallas as pl
from jax.experimental.pallas import tpu as pltpu
from jax.sharding import Mesh, PartitionSpec as P


MODES = 4
SEGS = 8
LANES = 128
TOGETHER = 2
MIX_WIDTH = 512
VMEM_LIMIT = 16 * 1024 * 1024


def shifted(x, amount, row):
    rolled = pltpu.roll(x, amount % SEGS, axis=0)
    inside = row >= amount if amount > 0 else row < SEGS + amount
    return jnp.where(inside, rolled, 0.0)


def segment_scan(x, factor, direction, row):
    total = shifted(x, direction, row)
    step = 1
    while step < SEGS:
        total = total + factor * shifted(total, direction * step, row)
        factor = factor * factor
        step *= 2
    return total


def columns(block):
    return pl.ds(pl.multiple_of(block * LANES, LANES), LANES)


def over_blocks(count, one):
    def trip(step, carry):
        for k in range(TOGETHER):
            one(step * TOGETHER + k, k)
        return carry

    lax.fori_loop(0, count // TOGETHER, trip, 0)


def spread_out(ref, n, cols):
    return jnp.broadcast_to(ref[n : n + 1, cols], (SEGS, LANES))


def mode_weights(decay, residue, cols):
    a = [spread_out(decay, n, cols) for n in range(MODES)]
    return a, [spread_out(residue, n, cols) * jnp.sqrt((1.0 - x) * (1.0 + x)) for n, x in enumerate(a)]


def squared(x, times):
    for _ in range(times):
        x = x * x
    return x


def loaded(query, key, value, cotangent, inner_buf, grad_buf, block, cols):
    inner_buf[block] = key[:, cols].astype(jnp.float32) * value[:, cols].astype(jnp.float32)
    grad_buf[block] = cotangent[:, cols].astype(jnp.float32) * query[:, cols].astype(jnp.float32)


def summarize(
    query, key, value, cotangent, decay_away,
    summary, query_held, key_held, value_held, cotangent_held, inner_buf, grad_buf, decay, arrived,
):
    tokens, width = query.shape
    steps = tokens // SEGS
    held = (query_held, key_held, value_held, cotangent_held)
    row = lax.broadcasted_iota(jnp.int32, (SEGS, LANES), 0)
    zero = jnp.zeros((SEGS, LANES), jnp.float32)

    copies = [
        pltpu.make_async_copy(ref, to, arrived.at[n])
        for n, (ref, to) in enumerate(zip((decay_away, query, key, value, cotangent), (decay, *held)))
    ]
    for copy in copies:
        copy.start()
    for copy in copies:
        copy.wait()

    def one(block, buf):
        cols = columns(block)
        loaded(*held, inner_buf, grad_buf, buf, cols)
        a = [spread_out(decay, n, cols) for n in range(MODES)]
        state, back, product, plain = [zero] * MODES, [zero] * MODES, [zero] * MODES, zero
        power = [zero + 1.0] * MODES
        for i in range(steps):
            u = inner_buf[buf, pl.ds(i, SEGS, stride=steps), :]
            g = grad_buf[buf, pl.ds(i, SEGS, stride=steps), :]
            plain = plain + g * u
            for n in range(MODES):
                state[n] = a[n] * state[n] + u
                product[n] = product[n] + g * state[n]
                back[n] = back[n] + power[n] * g
                power[n] = power[n] * a[n]
        for n in range(MODES):
            factor = power[n]
            before = segment_scan(state[n], factor, 1, row)
            after = segment_scan(back[n], factor, -1, row)
            summary[block, n : n + 1] = (factor * before + state[n])[SEGS - 1 :]
            summary[block, MODES + n : MODES + n + 1] = (factor * after + back[n])[:1]
            summary[block, 2 * MODES + n : 2 * MODES + n + 1] = jnp.sum(
                product[n] + a[n] * back[n] * before, axis=0, keepdims=True
            )
        summary[block, 3 * MODES : 3 * MODES + 1] = jnp.sum(plain, axis=0, keepdims=True)
        summary[block, 3 * MODES + 1 :] = jnp.zeros((MODES - 1, LANES), jnp.float32)

    over_blocks(width // LANES, one)


def mix(
    query, key, value, cotangent, decay, residue, skip,
    forward, backward, entered, left, decays, inner_buf, grad_buf,
):
    steps = forward.shape[0]
    doublings = steps.bit_length() - 1
    row = lax.broadcasted_iota(jnp.int32, (SEGS, LANES), 0)
    zero = jnp.zeros((SEGS, LANES), jnp.float32)
    for block in range(forward.shape[2] // LANES):
        cols = slice(block * LANES, (block + 1) * LANES)
        loaded(query, key, value, cotangent, inner_buf, grad_buf, block, cols)
        a, coef = mode_weights(decay, residue, cols)
        direct = spread_out(skip, 0, cols)
        state, back = [zero] * MODES, [zero] * MODES
        for i in range(steps):
            u = inner_buf[block, pl.ds(i, SEGS, stride=steps), :]
            mixed = direct * u
            for n in range(MODES):
                state[n] = a[n] * state[n] + u
                mixed = mixed + coef[n] * state[n]
            forward[i, :, cols] = mixed
        for i in reversed(range(steps)):
            g = grad_buf[block, pl.ds(i, SEGS, stride=steps), :]
            mixed = direct * g
            for n in range(MODES):
                back[n] = a[n] * back[n] + g
                mixed = mixed + coef[n] * back[n]
            backward[i, :, cols] = mixed
        for n in range(MODES):
            factor = squared(a[n], doublings)
            first = coef[n] * a[n]
            entered[n, :, cols] = first * segment_scan(state[n], factor, 1, row)
            left[n, :, cols] = first * segment_scan(back[n], factor, -1, row)
        decays[block] = decay[:, cols]


def finish(
    query, key, value, cotangent, decay, residue, carried,
    forward, backward, entered, left,
    output, query_grad, key_grad, value_grad, residue_grad, skip_grad, mixed_buf, back_buf,
):
    steps = forward.shape[0]
    doublings = steps.bit_length() - 1
    row = lax.broadcasted_iota(jnp.int32, (SEGS, LANES), 0)
    for block in range(forward.shape[2] // LANES):
        cols = slice(block * LANES, (block + 1) * LANES)
        a, coef = mode_weights(decay, residue, cols)
        ahead, behind = [], []
        for n in range(MODES):
            first = coef[n] * a[n]
            factor = squared(a[n], doublings)
            falling, rising = 1.0, 1.0
            for bit in (1, 2, 4):
                falling = falling * jnp.where(row & bit != 0, factor, 1.0)
                rising = rising * jnp.where(row & bit != 0, 1.0, factor)
                factor = factor * factor
            carry_in = jnp.broadcast_to(carried[block, n : n + 1], (SEGS, LANES))
            carry_back = jnp.broadcast_to(carried[block, MODES + n : MODES + n + 1], (SEGS, LANES))
            ahead.append(entered[n, :, cols] + first * falling * carry_in)
            behind.append(left[n, :, cols] + first * rising * carry_back)
        for i in range(steps):
            mixed = forward[i, :, cols]
            for n in range(MODES):
                mixed = mixed + ahead[n]
                ahead[n] = ahead[n] * a[n]
            mixed_buf[block, pl.ds(i, SEGS, stride=steps), :] = mixed
        for i in reversed(range(steps)):
            mixed = backward[i, :, cols]
            for n in range(MODES):
                mixed = mixed + behind[n]
                behind[n] = behind[n] * a[n]
            back_buf[block, pl.ds(i, SEGS, stride=steps), :] = mixed
        mixed_z = mixed_buf[block]
        inner_grad = back_buf[block]
        output[:, cols] = (query[:, cols].astype(jnp.float32) * mixed_z).astype(output.dtype)
        query_grad[:, cols] = (cotangent[:, cols].astype(jnp.float32) * mixed_z).astype(output.dtype)
        key_grad[:, cols] = (inner_grad * value[:, cols].astype(jnp.float32)).astype(output.dtype)
        value_grad[:, cols] = (inner_grad * key[:, cols].astype(jnp.float32)).astype(output.dtype)
        residue_grad[:, cols] = carried[block, 2 * MODES : 3 * MODES]
        skip_grad[:, cols] = carried[block, 3 * MODES : 3 * MODES + 1]


def rows_spec(rows):
    return pl.BlockSpec((rows, MIX_WIDTH), lambda i: (0, i))


def deep_spec(depth):
    return pl.BlockSpec((depth, SEGS, MIX_WIDTH), lambda i: (0, 0, i))


def per_block(rows):
    return pl.BlockSpec((MIX_WIDTH // LANES, rows, LANES), lambda i: (i, 0, 0))


def parts_of(gathered):
    return (
        gathered[:, :MODES],
        gathered[:, MODES : 2 * MODES],
        gathered[:, 2 * MODES : 3 * MODES],
        gathered[:, 3 * MODES : 3 * MODES + 1],
    )


def running(each, spans, reverse):
    step = 1
    for span in spans:
        rest = jnp.zeros((step, *each.shape[1:]), each.dtype)
        moved = jnp.concatenate([each[step:], rest] if reverse else [rest, each[:-step]], axis=0)
        each = each + span * moved
        step *= 2
    return each


def whole_of(parts, decay, spans):
    tails, heads, products, plains = parts
    count = tails.shape[0]
    tail, head, product, plain = tails[0], heads[count - 1], products[0], plains[0]
    for j in range(1, count):
        product = product + products[j] + decay * heads[j] * tail
        plain = plain + plains[j]
        tail = spans[0] * tail + tails[j]
        head = spans[0] * head + heads[count - 1 - j]
    return tail, head, product, plain


def weighted(weights, each):
    total = weights[0] * each[0]
    for j in range(1, each.shape[0]):
        total = total + weights[j] * each[j]
    return total


def padded(parts):
    plain = parts[3]
    rest = jnp.zeros((*plain.shape[:-2], MODES - 1, LANES), plain.dtype)
    return jnp.concatenate([*parts, rest], axis=-2)


def exchanged(blocks, axis):
    return lax.all_to_all(blocks, axis, 0, 0, tiled=True)


def swapped(block, place):
    odd, upper = place % 2 == 1, place >= 2
    across = lax.ppermute(block, "z_hi", [(2, 0), (3, 1)])
    wrapped = lax.ppermute(block, "z_hi", [(3, 0), (2, 1)])
    low = lax.ppermute(block, "z_hi", [(0, 1), (1, 0)])
    pair = (jnp.where(odd, low, block), jnp.where(odd, block, low))
    answer = lax.ppermute(jnp.stack(pair), "z_hi", [(0, 2), (1, 3)])
    high = lax.ppermute(block, "z_hi", [(2, 3), (3, 2)])
    return [
        jnp.where(upper, answer[0], pair[0]),
        jnp.where(upper, answer[1], pair[1]),
        jnp.where(upper, jnp.where(odd, high, block), jnp.where(odd, wrapped, across)),
        jnp.where(upper, jnp.where(odd, block, high), jnp.where(odd, across, wrapped)),
    ]


def local(query, key, value, cotangent, decay, residue, skip):
    tokens, width = query.shape
    steps = tokens // SEGS
    grid = (width // MIX_WIDTH,)
    wide, modes = rows_spec(tokens), rows_spec(MODES)
    shape_of, f32 = jax.ShapeDtypeStruct, jnp.float32
    buffers = [pltpu.VMEM((MIX_WIDTH // LANES, tokens, LANES), f32)] * 2
    small = pltpu.CompilerParams(vmem_limit_bytes=VMEM_LIMIT)
    far_off, whole = pl.BlockSpec(memory_space=pltpu.HBM), pl.BlockSpec(memory_space=pltpu.VMEM)
    blocks = width // LANES
    away = [pltpu.with_memory_space_constraint(x, pltpu.HBM) for x in (query, key, value, cotangent, decay)]
    summary, *sources = pl.pallas_call(
        summarize,
        in_specs=[far_off] * 5,
        out_specs=[whole] * 5,
        out_shape=[shape_of((blocks, 4 * MODES, LANES), f32)] + [pltpu.VMEM((tokens, width), query.dtype)] * 4,
        scratch_shapes=[pltpu.VMEM((TOGETHER, tokens, LANES), f32)] * 2
        + [pltpu.VMEM((MODES, width), f32), pltpu.SemaphoreType.DMA((5,))],
        compiler_params=small,
        name="summarize",
    )(*away)
    deep = [steps, steps, MODES, MODES]
    forward, backward, entered, left, decays = pl.pallas_call(
        mix,
        grid=grid,
        in_specs=[wide] * 4 + [modes] * 2 + [rows_spec(1)],
        out_specs=[deep_spec(depth) for depth in deep]
        + [per_block(MODES)],
        out_shape=[shape_of((depth, SEGS, width), f32) for depth in deep] + [shape_of((blocks, MODES, LANES), f32)],
        scratch_shapes=buffers,
        compiler_params=small,
        cost_estimate=pl.CostEstimate(flops=40 * tokens * width, bytes_accessed=16 * tokens * width, transcendentals=0),
        name="mix",
    )(*sources, decay, residue, skip[None, :])

    near = ("z_lo", "core")
    own_decay = lax.dynamic_index_in_dim(decays, lax.axis_index(near), 0, False)
    log_decay = jnp.log1p(own_decay - 1.0)

    def power(counts):
        return jnp.exp(counts[:, None, None] * log_decay)

    def held(used, counts):
        return jnp.where(used[:, None, None], power(jnp.maximum(counts, 0).astype(f32)), 0.0)

    near_count = lax.axis_size(near)
    mid_count, far_count = lax.axis_size("z_hi"), lax.axis_size("y")
    mid_place, far_place = lax.axis_index("z_hi"), lax.axis_index("y")
    mid_length = tokens * near_count
    far_length = mid_length * mid_count
    near_place = jnp.arange(near_count)
    reach_in = power((tokens * near_place).astype(f32))
    reach_back = power((tokens * (near_count - 1 - near_place)).astype(f32))
    doublings = (near_count * mid_count * far_count).bit_length() - 1
    spans = power((tokens * (1 << jnp.arange(doublings))).astype(f32))
    near_steps = near_count.bit_length() - 1
    mid_steps = near_steps + mid_count.bit_length() - 1
    mid = jnp.arange(mid_count)
    mid_in = held(mid < mid_place, mid_length * (mid_place - 1 - mid))
    mid_back = held(mid > mid_place, mid_length * (mid - mid_place - 1))
    far = jnp.arange(far_count)
    far_in = held(far < far_place, far_length * (far_place - 1 - far) + mid_length * mid_place)
    far_back = held(far > far_place, far_length * (far - far_place - 1) + mid_length * (mid_count - 1 - mid_place))
    scale = 1.0 / math.sqrt(far_length * far_count)
    spread = jnp.sqrt((1.0 - own_decay) * (1.0 + own_decay)) * scale

    def shared(stretch, count, axis):
        return parts_of(exchanged(jnp.broadcast_to(padded(stretch)[None], (count, 4 * MODES, LANES)), axis))

    near_parts = exchanged(summary, near)
    (
        near_parts, forward, backward, entered, left, own_decay, spread,
        reach_in, reach_back, spans, mid_in, mid_back, far_in, far_back,
    ) = lax.optimization_barrier(
        (
            near_parts, forward, backward, entered, left, own_decay, spread,
            reach_in, reach_back, [spans[k] for k in range(doublings)], mid_in, mid_back, far_in, far_back,
        )
    )
    near_spans, mid_spans, far_spans = spans[:near_steps], spans[near_steps:mid_steps], spans[mid_steps:]
    parts = parts_of(near_parts)
    ahead, behind = running(parts[0], near_spans, False), running(parts[1], near_spans, True)
    rest = jnp.zeros((1, MODES, LANES), f32)
    near_before = jnp.concatenate([rest, ahead[:-1]], axis=0)
    near_after = jnp.concatenate([behind[1:], rest], axis=0)
    products = jnp.sum(parts[2] + own_decay * parts[1] * near_before, axis=0)
    stretch = (ahead[-1], behind[0], products, jnp.sum(parts[3], axis=0))
    near_before, near_after, stretch = lax.optimization_barrier((near_before, near_after, stretch))
    parts = parts_of(jnp.stack(swapped(padded(stretch), mid_place)))
    entering, leaving = weighted(mid_in, parts[0]), weighted(mid_back, parts[1])
    stretch = whole_of(parts, own_decay, mid_spans)
    entering, leaving, stretch = lax.optimization_barrier((entering, leaving, stretch))
    parts = shared(stretch, far_count, "y")
    entering = entering + weighted(far_in, parts[0])
    leaving = leaving + weighted(far_back, parts[1])
    _, _, products, plain = whole_of(parts, own_decay, far_spans)
    everyone = (near_count, MODES, LANES)
    carried = padded(
        (
            near_before + reach_in * entering,
            near_after + reach_back * leaving,
            jnp.broadcast_to(spread * products, everyone),
            jnp.broadcast_to(scale * plain, (near_count, 1, LANES)),
        )
    )
    carried = exchanged(carried, near)

    bf16 = shape_of((tokens, width), query.dtype)
    *grads, skip_grad = pl.pallas_call(
        finish,
        grid=grid,
        in_specs=[wide] * 4 + [modes] * 2 + [per_block(4 * MODES)] + [deep_spec(depth) for depth in deep],
        out_specs=[wide] * 4 + [modes, rows_spec(1)],
        out_shape=[bf16] * 4 + [shape_of((MODES, width), f32), shape_of((1, width), f32)],
        scratch_shapes=buffers,
        compiler_params=small,
        name="finish",
    )(*sources, decay, residue, carried, forward, backward, entered, left)
    return (*grads, skip_grad[0])


def solution(mesh):
    context = ("y", "z_hi", "z_lo", "core")
    rows, columns = mesh.devices.shape
    fine = Mesh(mesh.devices.reshape(rows // 32, 4, 4, 2, columns), (*context, "ch"))
    wide, modes, flat = P(context, "ch"), P(None, "ch"), P("ch")
    return jax.shard_map(
        local,
        mesh=fine,
        in_specs=(wide, wide, wide, wide, modes, modes, flat),
        out_specs=(wide, wide, wide, wide, modes, flat),
        check_vma=False,
    )
```

```python
import math

import jax
import jax.numpy as jnp
from jax import lax
from jax.experimental import pallas as pl
from jax.experimental.pallas import tpu as pltpu
from jax.sharding import Mesh, PartitionSpec as P


MODES = 4
SEGS = 8
LANES = 128
TOGETHER = 2
MIX_WIDTH = 512
VMEM_LIMIT = 16 * 1024 * 1024


def shifted(x, amount, row):
    rolled = pltpu.roll(x, amount % SEGS, axis=0)
    inside = row >= amount if amount > 0 else row < SEGS + amount
    return jnp.where(inside, rolled, 0.0)


def segment_scan(x, factor, direction, row):
    total = shifted(x, direction, row)
    step = 1
    while step < SEGS:
        total = total + factor * shifted(total, direction * step, row)
        factor = factor * factor
        step *= 2
    return total


def columns(block):
    return pl.ds(pl.multiple_of(block * LANES, LANES), LANES)


def over_blocks(count, one):
    def trip(step, carry):
        for k in range(TOGETHER):
            one(step * TOGETHER + k, k)
        return carry

    lax.fori_loop(0, count // TOGETHER, trip, 0)


def spread_out(ref, n, cols):
    return jnp.broadcast_to(ref[n : n + 1, cols], (SEGS, LANES))


def mode_weights(decay, residue, cols):
    a = [spread_out(decay, n, cols) for n in range(MODES)]
    return a, [spread_out(residue, n, cols) * jnp.sqrt((1.0 - x) * (1.0 + x)) for n, x in enumerate(a)]


def squared(x, times):
    for _ in range(times):
        x = x * x
    return x


def loaded(query, key, value, cotangent, inner_buf, grad_buf, block, cols):
    inner_buf[block] = key[:, cols].astype(jnp.float32) * value[:, cols].astype(jnp.float32)
    grad_buf[block] = cotangent[:, cols].astype(jnp.float32) * query[:, cols].astype(jnp.float32)


def summarize(
    query, key, value, cotangent, decay_away,
    summary, query_held, key_held, value_held, cotangent_held, inner_buf, grad_buf, decay, arrived,
):
    tokens, width = query.shape
    steps = tokens // SEGS
    held = (query_held, key_held, value_held, cotangent_held)
    row = lax.broadcasted_iota(jnp.int32, (SEGS, LANES), 0)
    zero = jnp.zeros((SEGS, LANES), jnp.float32)

    copies = [
        pltpu.make_async_copy(ref, to, arrived.at[n])
        for n, (ref, to) in enumerate(zip((decay_away, query, key, value, cotangent), (decay, *held)))
    ]
    for copy in copies:
        copy.start()
    for copy in copies:
        copy.wait()

    def one(block, buf):
        cols = columns(block)
        loaded(*held, inner_buf, grad_buf, buf, cols)
        a = [spread_out(decay, n, cols) for n in range(MODES)]
        state, back, product, plain = [zero] * MODES, [zero] * MODES, [zero] * MODES, zero
        power = [zero + 1.0] * MODES
        for i in range(steps):
            u = inner_buf[buf, pl.ds(i, SEGS, stride=steps), :]
            g = grad_buf[buf, pl.ds(i, SEGS, stride=steps), :]
            plain = plain + g * u
            for n in range(MODES):
                state[n] = a[n] * state[n] + u
                product[n] = product[n] + g * state[n]
                back[n] = back[n] + power[n] * g
                power[n] = power[n] * a[n]
        for n in range(MODES):
            factor = power[n]
            before = segment_scan(state[n], factor, 1, row)
            after = segment_scan(back[n], factor, -1, row)
            summary[block, n : n + 1] = (factor * before + state[n])[SEGS - 1 :]
            summary[block, MODES + n : MODES + n + 1] = (factor * after + back[n])[:1]
            summary[block, 2 * MODES + n : 2 * MODES + n + 1] = jnp.sum(
                product[n] + a[n] * back[n] * before, axis=0, keepdims=True
            )
        summary[block, 3 * MODES : 3 * MODES + 1] = jnp.sum(plain, axis=0, keepdims=True)
        summary[block, 3 * MODES + 1 :] = jnp.zeros((MODES - 1, LANES), jnp.float32)

    over_blocks(width // LANES, one)


def mix(
    query, key, value, cotangent, decay, residue, skip,
    forward, backward, entered, left, decays, inner_buf, grad_buf,
):
    steps = forward.shape[0]
    doublings = steps.bit_length() - 1
    row = lax.broadcasted_iota(jnp.int32, (SEGS, LANES), 0)
    zero = jnp.zeros((SEGS, LANES), jnp.float32)
    for block in range(forward.shape[2] // LANES):
        cols = slice(block * LANES, (block + 1) * LANES)
        loaded(query, key, value, cotangent, inner_buf, grad_buf, block, cols)
        a, coef = mode_weights(decay, residue, cols)
        direct = spread_out(skip, 0, cols)
        state, back = [zero] * MODES, [zero] * MODES
        for i in range(steps):
            u = inner_buf[block, pl.ds(i, SEGS, stride=steps), :]
            mixed = direct * u
            for n in range(MODES):
                state[n] = a[n] * state[n] + u
                mixed = mixed + coef[n] * state[n]
            forward[i, :, cols] = mixed
        for i in reversed(range(steps)):
            g = grad_buf[block, pl.ds(i, SEGS, stride=steps), :]
            mixed = direct * g
            for n in range(MODES):
                back[n] = a[n] * back[n] + g
                mixed = mixed + coef[n] * back[n]
            backward[i, :, cols] = mixed
        for n in range(MODES):
            factor = squared(a[n], doublings)
            first = coef[n] * a[n]
            entered[n, :, cols] = first * segment_scan(state[n], factor, 1, row)
            left[n, :, cols] = first * segment_scan(back[n], factor, -1, row)
        decays[block] = decay[:, cols]


def finish(
    query, key, value, cotangent, decay, residue, carried,
    forward, backward, entered, left,
    output, query_grad, key_grad, value_grad, residue_grad, skip_grad, mixed_buf, back_buf,
):
    steps = forward.shape[0]
    doublings = steps.bit_length() - 1
    row = lax.broadcasted_iota(jnp.int32, (SEGS, LANES), 0)
    for block in range(forward.shape[2] // LANES):
        cols = slice(block * LANES, (block + 1) * LANES)
        a, coef = mode_weights(decay, residue, cols)
        ahead, behind = [], []
        for n in range(MODES):
            first = coef[n] * a[n]
            factor = squared(a[n], doublings)
            falling, rising = 1.0, 1.0
            for bit in (1, 2, 4):
                falling = falling * jnp.where(row & bit != 0, factor, 1.0)
                rising = rising * jnp.where(row & bit != 0, 1.0, factor)
                factor = factor * factor
            carry_in = jnp.broadcast_to(carried[block, n : n + 1], (SEGS, LANES))
            carry_back = jnp.broadcast_to(carried[block, MODES + n : MODES + n + 1], (SEGS, LANES))
            ahead.append(entered[n, :, cols] + first * falling * carry_in)
            behind.append(left[n, :, cols] + first * rising * carry_back)
        for i in range(steps):
            mixed = forward[i, :, cols]
            for n in range(MODES):
                mixed = mixed + ahead[n]
                ahead[n] = ahead[n] * a[n]
            mixed_buf[block, pl.ds(i, SEGS, stride=steps), :] = mixed
        for i in reversed(range(steps)):
            mixed = backward[i, :, cols]
            for n in range(MODES):
                mixed = mixed + behind[n]
                behind[n] = behind[n] * a[n]
            back_buf[block, pl.ds(i, SEGS, stride=steps), :] = mixed
        mixed_z = mixed_buf[block]
        inner_grad = back_buf[block]
        output[:, cols] = (query[:, cols].astype(jnp.float32) * mixed_z).astype(output.dtype)
        query_grad[:, cols] = (cotangent[:, cols].astype(jnp.float32) * mixed_z).astype(output.dtype)
        key_grad[:, cols] = (inner_grad * value[:, cols].astype(jnp.float32)).astype(output.dtype)
        value_grad[:, cols] = (inner_grad * key[:, cols].astype(jnp.float32)).astype(output.dtype)
        residue_grad[:, cols] = carried[block, 2 * MODES : 3 * MODES]
        skip_grad[:, cols] = carried[block, 3 * MODES : 3 * MODES + 1]


def rows_spec(rows):
    return pl.BlockSpec((rows, MIX_WIDTH), lambda i: (0, i))


def deep_spec(depth):
    return pl.BlockSpec((depth, SEGS, MIX_WIDTH), lambda i: (0, 0, i))


def per_block(rows):
    return pl.BlockSpec((MIX_WIDTH // LANES, rows, LANES), lambda i: (i, 0, 0))


def parts_of(gathered):
    return (
        gathered[:, :MODES],
        gathered[:, MODES : 2 * MODES],
        gathered[:, 2 * MODES : 3 * MODES],
        gathered[:, 3 * MODES : 3 * MODES + 1],
    )


def running(each, spans, reverse):
    step = 1
    for span in spans:
        rest = jnp.zeros((step, *each.shape[1:]), each.dtype)
        moved = jnp.concatenate([each[step:], rest] if reverse else [rest, each[:-step]], axis=0)
        each = each + span * moved
        step *= 2
    return each


def whole_of(parts, decay, spans):
    tails, heads, products, plains = parts
    count = tails.shape[0]
    tail, head, product, plain = tails[0], heads[count - 1], products[0], plains[0]
    for j in range(1, count):
        product = product + products[j] + decay * heads[j] * tail
        plain = plain + plains[j]
        tail = spans[0] * tail + tails[j]
        head = spans[0] * head + heads[count - 1 - j]
    return tail, head, product, plain


def weighted(weights, each):
    total = weights[0] * each[0]
    for j in range(1, each.shape[0]):
        total = total + weights[j] * each[j]
    return total


def padded(parts):
    plain = parts[3]
    rest = jnp.zeros((*plain.shape[:-2], MODES - 1, LANES), plain.dtype)
    return jnp.concatenate([*parts, rest], axis=-2)


def exchanged(blocks, axis, backwards=False):
    groups = [list(reversed(range(blocks.shape[0])))] if backwards else None
    return lax.all_to_all(blocks, axis, 0, 0, tiled=True, axis_index_groups=groups)


def swapped(block, place):
    odd, upper = place % 2 == 1, place >= 2
    across = lax.ppermute(block, "z_hi", [(2, 0), (3, 1)])
    wrapped = lax.ppermute(block, "z_hi", [(3, 0), (2, 1)])
    low = lax.ppermute(block, "z_hi", [(0, 1), (1, 0)])
    pair = (jnp.where(odd, low, block), jnp.where(odd, block, low))
    answer = lax.ppermute(jnp.stack(pair), "z_hi", [(0, 2), (1, 3)])
    high = lax.ppermute(block, "z_hi", [(2, 3), (3, 2)])
    return [
        jnp.where(upper, answer[0], pair[0]),
        jnp.where(upper, answer[1], pair[1]),
        jnp.where(upper, jnp.where(odd, high, block), jnp.where(odd, wrapped, across)),
        jnp.where(upper, jnp.where(odd, block, high), jnp.where(odd, across, wrapped)),
    ]


def local(query, key, value, cotangent, decay, residue, skip):
    tokens, width = query.shape
    steps = tokens // SEGS
    grid = (width // MIX_WIDTH,)
    wide, modes = rows_spec(tokens), rows_spec(MODES)
    shape_of, f32 = jax.ShapeDtypeStruct, jnp.float32
    buffers = [pltpu.VMEM((MIX_WIDTH // LANES, tokens, LANES), f32)] * 2
    small = pltpu.CompilerParams(vmem_limit_bytes=VMEM_LIMIT)
    far_off, whole = pl.BlockSpec(memory_space=pltpu.HBM), pl.BlockSpec(memory_space=pltpu.VMEM)
    blocks = width // LANES
    away = [pltpu.with_memory_space_constraint(x, pltpu.HBM) for x in (query, key, value, cotangent, decay)]
    summary, *sources = pl.pallas_call(
        summarize,
        in_specs=[far_off] * 5,
        out_specs=[whole] * 5,
        out_shape=[shape_of((blocks, 4 * MODES, LANES), f32)] + [pltpu.VMEM((tokens, width), query.dtype)] * 4,
        scratch_shapes=[pltpu.VMEM((TOGETHER, tokens, LANES), f32)] * 2
        + [pltpu.VMEM((MODES, width), f32), pltpu.SemaphoreType.DMA((5,))],
        compiler_params=small,
        name="summarize",
    )(*away)
    deep = [steps, steps, MODES, MODES]
    forward, backward, entered, left, decays = pl.pallas_call(
        mix,
        grid=grid,
        in_specs=[wide] * 4 + [modes] * 2 + [rows_spec(1)],
        out_specs=[deep_spec(depth) for depth in deep]
        + [per_block(MODES)],
        out_shape=[shape_of((depth, SEGS, width), f32) for depth in deep] + [shape_of((blocks, MODES, LANES), f32)],
        scratch_shapes=buffers,
        compiler_params=small,
        cost_estimate=pl.CostEstimate(flops=40 * tokens * width, bytes_accessed=16 * tokens * width, transcendentals=0),
        name="mix",
    )(*sources, decay, residue, skip[None, :])

    near = ("z_lo", "core")
    near_count = lax.axis_size(near)
    own_decay = lax.dynamic_index_in_dim(decays, near_count - 1 - lax.axis_index(near), 0, False)
    log_decay = jnp.log1p(own_decay - 1.0)

    def power(counts):
        return jnp.exp(counts[:, None, None] * log_decay)

    def held(used, counts):
        return jnp.where(used[:, None, None], power(jnp.maximum(counts, 0).astype(f32)), 0.0)

    mid_count, far_count = lax.axis_size("z_hi"), lax.axis_size("y")
    mid_place, far_place = lax.axis_index("z_hi"), lax.axis_index("y")
    mid_length = tokens * near_count
    far_length = mid_length * mid_count
    near_place = jnp.arange(near_count)
    reach_in = power((tokens * (near_count - 1 - near_place)).astype(f32))
    reach_back = power((tokens * near_place).astype(f32))
    doublings = (near_count * mid_count * far_count).bit_length() - 1
    spans = power((tokens * (1 << jnp.arange(doublings))).astype(f32))
    near_steps = near_count.bit_length() - 1
    mid_steps = near_steps + mid_count.bit_length() - 1
    mid = jnp.arange(mid_count)
    mid_in = held(mid < mid_place, mid_length * (mid_place - 1 - mid))
    mid_back = held(mid > mid_place, mid_length * (mid - mid_place - 1))
    far = jnp.arange(far_count)
    far_in = held(far < far_place, far_length * (far_place - 1 - far) + mid_length * mid_place)
    far_back = held(far > far_place, far_length * (far - far_place - 1) + mid_length * (mid_count - 1 - mid_place))
    scale = 1.0 / math.sqrt(far_length * far_count)
    spread = jnp.sqrt((1.0 - own_decay) * (1.0 + own_decay)) * scale

    def shared(stretch, count, axis):
        blocks = jnp.broadcast_to(padded(stretch)[None], (count, 4 * MODES, LANES))
        return parts_of(exchanged(blocks, axis, backwards=True)[::-1])

    near_parts = exchanged(summary, near, backwards=True)
    (
        near_parts, forward, backward, entered, left, own_decay, spread,
        reach_in, reach_back, spans, mid_in, mid_back, far_in, far_back,
    ) = lax.optimization_barrier(
        (
            near_parts, forward, backward, entered, left, own_decay, spread,
            reach_in, reach_back, [spans[k] for k in range(doublings)], mid_in, mid_back, far_in, far_back,
        )
    )
    near_spans, mid_spans, far_spans = spans[:near_steps], spans[near_steps:mid_steps], spans[mid_steps:]
    parts = parts_of(near_parts)
    ahead, behind = running(parts[0], near_spans, True), running(parts[1], near_spans, False)
    rest = jnp.zeros((1, MODES, LANES), f32)
    near_before = jnp.concatenate([ahead[1:], rest], axis=0)
    near_after = jnp.concatenate([rest, behind[:-1]], axis=0)
    products = jnp.sum(parts[2] + own_decay * parts[1] * near_before, axis=0)
    stretch = (ahead[0], behind[-1], products, jnp.sum(parts[3], axis=0))
    near_before, near_after, stretch = lax.optimization_barrier((near_before, near_after, stretch))
    parts = parts_of(jnp.stack(swapped(padded(stretch), mid_place)))
    entering, leaving = weighted(mid_in, parts[0]), weighted(mid_back, parts[1])
    stretch = whole_of(parts, own_decay, mid_spans)
    entering, leaving, stretch = lax.optimization_barrier((entering, leaving, stretch))
    parts = shared(stretch, far_count, "y")
    entering = entering + weighted(far_in, parts[0])
    leaving = leaving + weighted(far_back, parts[1])
    _, _, products, plain = whole_of(parts, own_decay, far_spans)
    everyone = (near_count, MODES, LANES)
    carried = padded(
        (
            near_before + reach_in * entering,
            near_after + reach_back * leaving,
            jnp.broadcast_to(spread * products, everyone),
            jnp.broadcast_to(scale * plain, (near_count, 1, LANES)),
        )
    )
    carried = exchanged(carried, near, backwards=True)

    bf16 = shape_of((tokens, width), query.dtype)
    *grads, skip_grad = pl.pallas_call(
        finish,
        grid=grid,
        in_specs=[wide] * 4 + [modes] * 2 + [per_block(4 * MODES)] + [deep_spec(depth) for depth in deep],
        out_specs=[wide] * 4 + [modes, rows_spec(1)],
        out_shape=[bf16] * 4 + [shape_of((MODES, width), f32), shape_of((1, width), f32)],
        scratch_shapes=buffers,
        compiler_params=small,
        name="finish",
    )(*sources, decay, residue, carried, forward, backward, entered, left)
    return (*grads, skip_grad[0])


def solution(mesh):
    context = ("y", "z_hi", "z_lo", "core")
    rows, columns = mesh.devices.shape
    fine = Mesh(mesh.devices.reshape(rows // 32, 4, 4, 2, columns), (*context, "ch"))
    wide, modes, flat = P(context, "ch"), P(None, "ch"), P("ch")
    return jax.shard_map(
        local,
        mesh=fine,
        in_specs=(wide, wide, wide, wide, modes, modes, flat),
        out_specs=(wide, wide, wide, wide, modes, flat),
        check_vma=False,
    )
```

```python
import math

import jax
import jax.numpy as jnp
from jax import lax
from jax.experimental import pallas as pl
from jax.experimental.pallas import tpu as pltpu
from jax.sharding import Mesh, PartitionSpec as P


MODES = 4
SEGS = 8
LANES = 128
TOGETHER = 2
LEAD = 4
MIX_WIDTH = 512
VMEM_LIMIT = 16 * 1024 * 1024


def shifted(x, amount, row):
    rolled = pltpu.roll(x, amount % SEGS, axis=0)
    inside = row >= amount if amount > 0 else row < SEGS + amount
    return jnp.where(inside, rolled, 0.0)


def segment_scan(x, factor, direction, row):
    total = shifted(x, direction, row)
    step = 1
    while step < SEGS:
        total = total + factor * shifted(total, direction * step, row)
        factor = factor * factor
        step *= 2
    return total


def columns(block):
    return pl.ds(pl.multiple_of(block * LANES, LANES), LANES)


def over_blocks(count, one):
    def trip(step, carry):
        for k in range(TOGETHER):
            one(step * TOGETHER + k, k)
        return carry

    lax.fori_loop(0, count // TOGETHER, trip, 0)


def spread_out(ref, n, cols):
    return jnp.broadcast_to(ref[n : n + 1, cols], (SEGS, LANES))


def mode_weights(decay, residue, cols):
    a = [spread_out(decay, n, cols) for n in range(MODES)]
    return a, [spread_out(residue, n, cols) * jnp.sqrt((1.0 - x) * (1.0 + x)) for n, x in enumerate(a)]


def squared(x, times):
    for _ in range(times):
        x = x * x
    return x


def loaded(query, key, value, cotangent, inner_buf, grad_buf, block, cols):
    inner_buf[block] = key[:, cols].astype(jnp.float32) * value[:, cols].astype(jnp.float32)
    grad_buf[block] = cotangent[:, cols].astype(jnp.float32) * query[:, cols].astype(jnp.float32)


def summarize(
    query, key, value, cotangent, decay_away,
    summary, query_held, key_held, value_held, cotangent_held, inner_buf, grad_buf, decay, arrived,
):
    tokens, width = query.shape
    steps = tokens // SEGS
    held = (query_held, key_held, value_held, cotangent_held)
    row = lax.broadcasted_iota(jnp.int32, (SEGS, LANES), 0)
    zero = jnp.zeros((SEGS, LANES), jnp.float32)

    copies = [
        pltpu.make_async_copy(ref, to, arrived.at[n])
        for n, (ref, to) in enumerate(zip((decay_away, query, key, value, cotangent), (decay, *held)))
    ]
    for copy in copies:
        copy.start()
    for copy in copies:
        copy.wait()

    def one(block, buf):
        cols = columns(block)
        loaded(*held, inner_buf, grad_buf, buf, cols)
        a = [spread_out(decay, n, cols) for n in range(MODES)]
        state, back, product, plain = [zero] * MODES, [zero] * MODES, [zero] * MODES, zero
        power = [zero + 1.0] * MODES
        for i in range(steps):
            u = inner_buf[buf, pl.ds(i, SEGS, stride=steps), :]
            g = grad_buf[buf, pl.ds(i, SEGS, stride=steps), :]
            plain = plain + g * u
            for n in range(MODES):
                state[n] = a[n] * state[n] + u
                product[n] = product[n] + g * state[n]
                back[n] = back[n] + power[n] * g
                power[n] = power[n] * a[n]
        for n in range(MODES):
            factor = power[n]
            before = segment_scan(state[n], factor, 1, row)
            after = segment_scan(back[n], factor, -1, row)
            summary[block, n : n + 1] = (factor * before + state[n])[SEGS - 1 :]
            summary[block, MODES + n : MODES + n + 1] = (factor * after + back[n])[:1]
            summary[block, 2 * MODES + n : 2 * MODES + n + 1] = jnp.sum(
                product[n] + a[n] * back[n] * before, axis=0, keepdims=True
            )
        summary[block, 3 * MODES : 3 * MODES + 1] = jnp.sum(plain, axis=0, keepdims=True)
        summary[block, 3 * MODES + 1 :] = jnp.zeros((MODES - 1, LANES), jnp.float32)

    over_blocks(width // LANES, one)


def mix(
    query, key, value, cotangent, decay, residue, skip,
    forward, backward, entered, left, decays, inner_buf, grad_buf,
):
    steps = forward.shape[0]
    doublings = steps.bit_length() - 1
    row = lax.broadcasted_iota(jnp.int32, (SEGS, LANES), 0)
    zero = jnp.zeros((SEGS, LANES), jnp.float32)
    for block in range(forward.shape[2] // LANES):
        cols = slice(block * LANES, (block + 1) * LANES)
        loaded(query, key, value, cotangent, inner_buf, grad_buf, block, cols)
        a, coef = mode_weights(decay, residue, cols)
        direct = spread_out(skip, 0, cols)
        state, back = [zero] * MODES, [zero] * MODES
        for i in range(steps):
            u = inner_buf[block, pl.ds(i, SEGS, stride=steps), :]
            mixed = direct * u
            for n in range(MODES):
                state[n] = a[n] * state[n] + u
                mixed = mixed + coef[n] * state[n]
            forward[i, :, cols] = mixed
        for i in reversed(range(steps)):
            g = grad_buf[block, pl.ds(i, SEGS, stride=steps), :]
            mixed = direct * g
            for n in range(MODES):
                back[n] = a[n] * back[n] + g
                mixed = mixed + coef[n] * back[n]
            backward[i, :, cols] = mixed
        for n in range(MODES):
            factor = squared(a[n], doublings)
            first = coef[n] * a[n]
            entered[n, :, cols] = first * segment_scan(state[n], factor, 1, row)
            left[n, :, cols] = first * segment_scan(back[n], factor, -1, row)
        decays[block] = decay[:, cols]


def finish(
    query, key, value, cotangent, decay, residue, carried,
    forward, backward, entered, left,
    output, query_grad, key_grad, value_grad, residue_grad, skip_grad, mixed_buf, back_buf,
):
    steps = forward.shape[0]
    doublings = steps.bit_length() - 1
    row = lax.broadcasted_iota(jnp.int32, (SEGS, LANES), 0)
    for block in range(forward.shape[2] // LANES):
        cols = slice(block * LANES, (block + 1) * LANES)
        a, coef = mode_weights(decay, residue, cols)
        ahead, behind = [], []
        for n in range(MODES):
            first = coef[n] * a[n]
            factor = squared(a[n], doublings)
            falling, rising = 1.0, 1.0
            for bit in (1, 2, 4):
                falling = falling * jnp.where(row & bit != 0, factor, 1.0)
                rising = rising * jnp.where(row & bit != 0, 1.0, factor)
                factor = factor * factor
            carry_in = jnp.broadcast_to(carried[block, n : n + 1], (SEGS, LANES))
            carry_back = jnp.broadcast_to(carried[block, MODES + n : MODES + n + 1], (SEGS, LANES))
            ahead.append(entered[n, :, cols] + first * falling * carry_in)
            behind.append(left[n, :, cols] + first * rising * carry_back)
        for i in range(steps):
            mixed = forward[i, :, cols]
            for n in range(MODES):
                mixed = mixed + ahead[n]
                ahead[n] = ahead[n] * a[n]
            mixed_buf[block, pl.ds(i, SEGS, stride=steps), :] = mixed
        for i in reversed(range(steps)):
            mixed = backward[i, :, cols]
            for n in range(MODES):
                mixed = mixed + behind[n]
                behind[n] = behind[n] * a[n]
            back_buf[block, pl.ds(i, SEGS, stride=steps), :] = mixed
        mixed_z = mixed_buf[block]
        inner_grad = back_buf[block]
        output[:, cols] = (query[:, cols].astype(jnp.float32) * mixed_z).astype(output.dtype)
        query_grad[:, cols] = (cotangent[:, cols].astype(jnp.float32) * mixed_z).astype(output.dtype)
        key_grad[:, cols] = (inner_grad * value[:, cols].astype(jnp.float32)).astype(output.dtype)
        value_grad[:, cols] = (inner_grad * key[:, cols].astype(jnp.float32)).astype(output.dtype)
        residue_grad[:, cols] = carried[block, 2 * MODES : 3 * MODES]
        skip_grad[:, cols] = carried[block, 3 * MODES : 3 * MODES + 1]


def rows_spec(rows):
    return pl.BlockSpec((rows, MIX_WIDTH), lambda i: (0, i))


def deep_spec(depth):
    return pl.BlockSpec((depth, SEGS, MIX_WIDTH), lambda i: (0, 0, i))


def per_block(rows):
    return pl.BlockSpec((MIX_WIDTH // LANES, rows, LANES), lambda i: (i, 0, 0))


def parts_of(gathered):
    return (
        gathered[:, :MODES],
        gathered[:, MODES : 2 * MODES],
        gathered[:, 2 * MODES : 3 * MODES],
        gathered[:, 3 * MODES : 3 * MODES + 1],
    )


def running(each, spans, reverse):
    step = 1
    for span in spans:
        rest = jnp.zeros((step, *each.shape[1:]), each.dtype)
        moved = jnp.concatenate([each[step:], rest] if reverse else [rest, each[:-step]], axis=0)
        each = each + span * moved
        step *= 2
    return each


def whole_of(parts, decay, spans):
    tails, heads, products, plains = parts
    count = tails.shape[0]
    tail, head, product, plain = tails[0], heads[count - 1], products[0], plains[0]
    for j in range(1, count):
        product = product + products[j] + decay * heads[j] * tail
        plain = plain + plains[j]
        tail = spans[0] * tail + tails[j]
        head = spans[0] * head + heads[count - 1 - j]
    return tail, head, product, plain


def weighted(weights, each):
    total = weights[0] * each[0]
    for j in range(1, each.shape[0]):
        total = total + weights[j] * each[j]
    return total


def padded(parts):
    plain = parts[3]
    rest = jnp.zeros((*plain.shape[:-2], MODES - 1, LANES), plain.dtype)
    return jnp.concatenate([*parts, rest], axis=-2)


def exchanged(blocks, axis, order):
    return lax.all_to_all(blocks, axis, 0, 0, tiled=True, axis_index_groups=[order])


def swapped(block, place):
    odd, upper = place % 2 == 1, place >= 2
    across = lax.ppermute(block, "z_hi", [(2, 0), (3, 1)])
    wrapped = lax.ppermute(block, "z_hi", [(3, 0), (2, 1)])
    low = lax.ppermute(block, "z_hi", [(0, 1), (1, 0)])
    pair = (jnp.where(odd, low, block), jnp.where(odd, block, low))
    answer = lax.ppermute(jnp.stack(pair), "z_hi", [(0, 2), (1, 3)])
    high = lax.ppermute(block, "z_hi", [(2, 3), (3, 2)])
    return [
        jnp.where(upper, answer[0], pair[0]),
        jnp.where(upper, answer[1], pair[1]),
        jnp.where(upper, jnp.where(odd, high, block), jnp.where(odd, wrapped, across)),
        jnp.where(upper, jnp.where(odd, block, high), jnp.where(odd, across, wrapped)),
    ]


def local(query, key, value, cotangent, decay, residue, skip):
    tokens, width = query.shape
    steps = tokens // SEGS
    grid = (width // MIX_WIDTH,)
    wide, modes = rows_spec(tokens), rows_spec(MODES)
    shape_of, f32 = jax.ShapeDtypeStruct, jnp.float32
    buffers = [pltpu.VMEM((MIX_WIDTH // LANES, tokens, LANES), f32)] * 2
    small = pltpu.CompilerParams(vmem_limit_bytes=VMEM_LIMIT)
    far_off, whole = pl.BlockSpec(memory_space=pltpu.HBM), pl.BlockSpec(memory_space=pltpu.VMEM)
    blocks = width // LANES
    away = [pltpu.with_memory_space_constraint(x, pltpu.HBM) for x in (query, key, value, cotangent, decay)]
    summary, *sources = pl.pallas_call(
        summarize,
        in_specs=[far_off] * 5,
        out_specs=[whole] * 5,
        out_shape=[shape_of((blocks, 4 * MODES, LANES), f32)] + [pltpu.VMEM((tokens, width), query.dtype)] * 4,
        scratch_shapes=[pltpu.VMEM((TOGETHER, tokens, LANES), f32)] * 2
        + [pltpu.VMEM((MODES, width), f32), pltpu.SemaphoreType.DMA((5,))],
        compiler_params=small,
        name="summarize",
    )(*away)
    deep = [steps, steps, MODES, MODES]
    forward, backward, entered, left, decays = pl.pallas_call(
        mix,
        grid=grid,
        in_specs=[wide] * 4 + [modes] * 2 + [rows_spec(1)],
        out_specs=[deep_spec(depth) for depth in deep]
        + [per_block(MODES)],
        out_shape=[shape_of((depth, SEGS, width), f32) for depth in deep] + [shape_of((blocks, MODES, LANES), f32)],
        scratch_shapes=buffers,
        compiler_params=small,
        cost_estimate=pl.CostEstimate(flops=40 * tokens * width, bytes_accessed=16 * tokens * width, transcendentals=0),
        name="mix",
    )(*sources, decay, residue, skip[None, :])

    near = ("z_lo", "core")
    near_count = lax.axis_size(near)
    near_order = [(i + LEAD) % near_count for i in range(near_count)]
    own_chunk = lax.rem(lax.axis_index(near) + near_count - LEAD, near_count)
    own_decay = lax.dynamic_index_in_dim(decays, own_chunk, 0, False)
    log_decay = jnp.log1p(own_decay - 1.0)

    def power(counts):
        return jnp.exp(counts[:, None, None] * log_decay)

    def held(used, counts):
        return jnp.where(used[:, None, None], power(jnp.maximum(counts, 0).astype(f32)), 0.0)

    mid_count, far_count = lax.axis_size("z_hi"), lax.axis_size("y")
    mid_place, far_place = lax.axis_index("z_hi"), lax.axis_index("y")
    mid_length = tokens * near_count
    far_length = mid_length * mid_count
    near_place = (jnp.arange(near_count) + LEAD) % near_count
    reach_in = power((tokens * near_place).astype(f32))
    reach_back = power((tokens * (near_count - 1 - near_place)).astype(f32))
    doublings = (near_count * mid_count * far_count).bit_length() - 1
    spans = power((tokens * (1 << jnp.arange(doublings))).astype(f32))
    near_steps = near_count.bit_length() - 1
    mid_steps = near_steps + mid_count.bit_length() - 1
    mid = jnp.arange(mid_count)
    mid_in = held(mid < mid_place, mid_length * (mid_place - 1 - mid))
    mid_back = held(mid > mid_place, mid_length * (mid - mid_place - 1))
    far = jnp.arange(far_count)
    far_in = held(far < far_place, far_length * (far_place - 1 - far) + mid_length * mid_place)
    far_back = held(far > far_place, far_length * (far - far_place - 1) + mid_length * (mid_count - 1 - mid_place))
    scale = 1.0 / math.sqrt(far_length * far_count)
    spread = jnp.sqrt((1.0 - own_decay) * (1.0 + own_decay)) * scale

    def shared(stretch, count, axis):
        blocks = jnp.broadcast_to(padded(stretch)[None], (count, 4 * MODES, LANES))
        return parts_of(exchanged(blocks, axis, list(reversed(range(count))))[::-1])

    near_parts = exchanged(summary, near, near_order)
    (
        near_parts, forward, backward, entered, left, own_decay, spread,
        reach_in, reach_back, spans, mid_in, mid_back, far_in, far_back,
    ) = lax.optimization_barrier(
        (
            near_parts, forward, backward, entered, left, own_decay, spread,
            reach_in, reach_back, [spans[k] for k in range(doublings)], mid_in, mid_back, far_in, far_back,
        )
    )
    near_spans, mid_spans, far_spans = spans[:near_steps], spans[near_steps:mid_steps], spans[mid_steps:]
    parts = parts_of(jnp.roll(near_parts, LEAD, axis=0))
    ahead, behind = running(parts[0], near_spans, False), running(parts[1], near_spans, True)
    rest = jnp.zeros((1, MODES, LANES), f32)
    near_before = jnp.concatenate([rest, ahead[:-1]], axis=0)
    near_after = jnp.concatenate([behind[1:], rest], axis=0)
    products = jnp.sum(parts[2] + own_decay * parts[1] * near_before, axis=0)
    stretch = (ahead[-1], behind[0], products, jnp.sum(parts[3], axis=0))
    near_before, near_after = jnp.roll(near_before, -LEAD, axis=0), jnp.roll(near_after, -LEAD, axis=0)
    near_before, near_after, stretch = lax.optimization_barrier((near_before, near_after, stretch))
    parts = parts_of(jnp.stack(swapped(padded(stretch), mid_place)))
    entering, leaving = weighted(mid_in, parts[0]), weighted(mid_back, parts[1])
    stretch = whole_of(parts, own_decay, mid_spans)
    entering, leaving, stretch = lax.optimization_barrier((entering, leaving, stretch))
    parts = shared(stretch, far_count, "y")
    entering = entering + weighted(far_in, parts[0])
    leaving = leaving + weighted(far_back, parts[1])
    _, _, products, plain = whole_of(parts, own_decay, far_spans)
    everyone = (near_count, MODES, LANES)
    carried = padded(
        (
            near_before + reach_in * entering,
            near_after + reach_back * leaving,
            jnp.broadcast_to(spread * products, everyone),
            jnp.broadcast_to(scale * plain, (near_count, 1, LANES)),
        )
    )
    carried = exchanged(carried, near, near_order)

    bf16 = shape_of((tokens, width), query.dtype)
    *grads, skip_grad = pl.pallas_call(
        finish,
        grid=grid,
        in_specs=[wide] * 4 + [modes] * 2 + [per_block(4 * MODES)] + [deep_spec(depth) for depth in deep],
        out_specs=[wide] * 4 + [modes, rows_spec(1)],
        out_shape=[bf16] * 4 + [shape_of((MODES, width), f32), shape_of((1, width), f32)],
        scratch_shapes=buffers,
        compiler_params=small,
        name="finish",
    )(*sources, decay, residue, carried, forward, backward, entered, left)
    return (*grads, skip_grad[0])


def solution(mesh):
    context = ("y", "z_hi", "z_lo", "core")
    rows, columns = mesh.devices.shape
    fine = Mesh(mesh.devices.reshape(rows // 32, 4, 4, 2, columns), (*context, "ch"))
    wide, modes, flat = P(context, "ch"), P(None, "ch"), P("ch")
    return jax.shard_map(
        local,
        mesh=fine,
        in_specs=(wide, wide, wide, wide, modes, modes, flat),
        out_specs=(wide, wide, wide, wide, modes, flat),
        check_vma=False,
    )
```
